128 devices in a mesh: freq: 2 (over core), vs: 64 (over z, y, x).
Axes of the slice: x: 4, y: 4, z: 4, core: 2. Of those that a mesh axis runs over, the one named last changes fastest.
Arguments:
- kernel: bfloat16 [4, 2, 256, 16384], P('freq', None, None, 'vs'), may hold values from -0.03125 to 0.03125
- sources: bfloat16 [4, 2, 2048, 16384], P('freq', None, 'vs'), may hold values from -6 to 6
- observed: float32 [256, 160, 2048], P('freq', None, 'vs'), may hold values from -6 to 6
- gate_start: int32 [256], P('freq'), may hold values from 0 to 80, as said below
- gate_length: int32 [256], P('freq'), may hold values from 1 to 160
Outputs:
- gradient: bfloat16 [4, 2, 2048, 16384], P('freq', None, 'vs')
- misfit: float32 [256, 160, 2048], P('freq', None, 'vs')
The draws below stay inside these ranges and needn't reach their ends.
Inputs may be any that keep to these rules, and one draw needn't show every extreme that they name: gate_start + gate_length <= 160 for every receiver.
All inputs are finite; a program needn't handle non-finite values.
Results may differ from the reference program's by a relative error of at most 0.0057.
Values may be sent and summed in bfloat16 or wider, within the bound.
No kernel may reach another device: no remote copies, remote signals or barrier semaphores. Data moves between devices by JAX's collectives and lax.ppermute only.
A program may use at most 128 MiB of HBM per device.

```python
import jax
import jax.numpy as jnp
from jax import lax

NS = 16384
NT = 160
RW = 256
NF = 4
NV = 2048


def gate_pair(key):
    base_key = jax.random.fold_in(key, 4242)
    key_start, key_spread, key_reach, key_choose = jax.random.split(base_key, 4)
    row_index = jnp.arange(RW, dtype=jnp.int32)
    opening = jax.random.randint(key_start, (RW,), 0, NT // 2 + 1, dtype=jnp.int32)
    chosen = jax.random.randint(key_choose, (), 0, RW, dtype=jnp.int32)
    second_row = (chosen + RW // 2) % RW
    opening = jnp.where(row_index == chosen, 0, opening)
    opening = jnp.where(row_index == second_row, NT // 2, opening)
    spread = jax.random.randint(key_spread, (RW,), 0, 1 << 20, dtype=jnp.int32)
    finish = opening + 1 + spread % (NT - opening)
    reaches = jax.random.randint(key_reach, (RW,), 0, 4, dtype=jnp.int32) == 0
    finish = jnp.where(reaches | (row_index == chosen), NT, finish)
    return (opening, finish - opening)


def draw_gate_start(key, part):
    return gate_pair(key)[0]


def draw_gate_length(key, part):
    return gate_pair(key)[1]


def block_scale(own_key, extent, cuts, smallest, largest):
    def one(dim, blocks):
        steps = jax.random.uniform(jax.random.fold_in(jax.random.fold_in(own_key, 6), dim), (blocks,), jnp.float32, smallest / len(cuts), largest / len(cuts))
        return jnp.repeat(jnp.exp(steps), extent[dim] // blocks).reshape((-1,) + (1,) * (len(extent) - dim - 1))

    factor_of = one(*cuts[0])
    for cut in cuts[1:]:
        factor_of = factor_of * one(*cut)
    return factor_of


def centred(rng, extent, deviation, limit, cuts=(), held_as=jnp.bfloat16):
    drawn = jax.random.normal(rng, extent, jnp.float32) * deviation
    if len(cuts) > 0:
        drawn = block_scale(rng, extent, cuts, -0.22, 0.18) * drawn
    return jnp.clip(drawn, min=-limit, max=limit).astype(held_as)


def setup_inputs(seed: int = 0) -> dict:
    splits = jax.random.split(jax.random.key(seed), 6)
    kernel = centred(splits[0], (NF, 2, RW, NS), (2 * NS) ** -0.5, 0.03125, ((0, 2), (3, 64)))
    sources = centred(splits[1], (NF, 2, NV, NS), 1.0, 6.0, ((0, 2), (2, 64)))
    observed = centred(splits[2], (RW, NT, NV), 1.0, 6.0, ((0, 2), (2, 64)), jnp.float32)
    gate_start = draw_gate_start(jax.random.fold_in(splits[5], 71), 0)
    gate_length = draw_gate_length(jax.random.fold_in(splits[5], 71), 0)
    return dict(kernel=kernel, sources=sources, observed=observed, gate_start=gate_start, gate_length=gate_length)


def forward_one(pair):
    kern, model = pair
    real_part = jnp.dot(kern[0], model[0].T, preferred_element_type=jnp.float32) - jnp.dot(kern[1], model[1].T, preferred_element_type=jnp.float32)
    imag_part = jnp.dot(kern[0], model[1].T, preferred_element_type=jnp.float32) + jnp.dot(kern[1], model[0].T, preferred_element_type=jnp.float32)
    return jnp.stack([real_part, imag_part], 0).astype(jnp.bfloat16)


def adjoint_one(pair):
    kern, spectrum = pair
    real_part = jnp.dot(spectrum[0].T, kern[0], preferred_element_type=jnp.float32) + jnp.dot(spectrum[1].T, kern[1], preferred_element_type=jnp.float32)
    imag_part = jnp.dot(spectrum[1].T, kern[0], preferred_element_type=jnp.float32) - jnp.dot(spectrum[0].T, kern[1], preferred_element_type=jnp.float32)
    factor = (NS / RW) ** 0.5
    return (factor * jnp.stack([real_part, imag_part], 0)).astype(jnp.bfloat16)


def transform_tables(count, samples):
    sample_index = jnp.arange(samples, dtype=jnp.int32)
    bin_index = samples // 4 + jnp.arange(count, dtype=jnp.int32)
    phase = (sample_index[:, None] * bin_index[None, :]) % samples
    theta = (2.0 * jnp.pi / samples) * phase.astype(jnp.float32)
    return jnp.cos(theta), jnp.sin(theta)


def reference(kernel, sources, observed, gate_start, gate_length):
    field = lax.map(forward_one, (kernel, sources))
    count = field.shape[0]
    samples = observed.shape[1]
    cosine, sine = transform_tables(count, samples)
    scale = count ** -0.5
    values = field.astype(jnp.float32)
    highest = lax.Precision.HIGHEST
    signal = scale * (jnp.einsum("tf,frv->rtv", cosine, values[:, 0], precision=highest) - jnp.einsum("tf,frv->rtv", sine, values[:, 1], precision=highest))
    sample_index = jnp.arange(samples, dtype=jnp.int32)
    inside = (sample_index[None, :] >= gate_start[:, None]) & (sample_index[None, :] < (gate_start + gate_length)[:, None])
    gate_mask = inside.astype(jnp.float32)
    misfit = gate_mask[:, :, None] * (signal - observed)
    back_real = scale * jnp.einsum("tf,rtv->frv", cosine, misfit, precision=highest)
    back_imag = -scale * jnp.einsum("tf,rtv->frv", sine, misfit, precision=highest)
    back_spectrum = jnp.stack([back_real, back_imag], 1).astype(jnp.bfloat16)
    gradient = lax.map(adjoint_one, (kernel, back_spectrum))
    return gradient, misfit
```

```python
import functools

import jax
import jax.numpy as jnp
from jax import lax
from jax.experimental import pallas as pl
from jax.experimental.pallas import tpu as pltpu
from jax.sharding import Mesh, PartitionSpec as P


NS = 16384
RW = 256
SIDE = 4
BLOCK = 256
GROUP = 32
POINTS = 4096
OFFSETS = (0, -1, 1, 2)
EXCHANGE = ("x", "y")
PLANE = ("y", "x")
F32 = jnp.float32
BF16 = jnp.bfloat16


def ring_shift(value, axis, step):
    pairs = [(i, (i + step) % SIDE) for i in range(SIDE)]
    return lax.ppermute(value, axis, pairs)


def wrap(index, step):
    return lax.rem(index + (step + SIDE), SIDE)


def column(freq, z, plane, exchange):
    if freq == 0:
        block = (z * SIDE + plane) * SIDE + exchange
    else:
        block = (z * SIDE + exchange) * SIDE + plane
    return pl.multiple_of(block * BLOCK, BLOCK)


def call(body, out_shape, **kw):
    return pl.pallas_call(body, out_shape=out_shape, **kw)


def shape(dims, dtype):
    return jax.ShapeDtypeStruct(dims, dtype)


def pack_body(freq, x_ref, *outs):
    here = lax.axis_index(EXCHANGE[freq])
    for step, out in zip((0, 1, -1, 2), outs):
        there = wrap(here, step)
        for z in range(SIDE):
            for plane in range(SIDE):
                at = (z * SIDE + plane) * BLOCK
                src = column(freq, z, plane, there)
                out[0, :, at : at + BLOCK] = x_ref[0, 0, :, pl.ds(src, BLOCK)]


def pack(sources, freq):
    return call(
        functools.partial(pack_body, freq),
        [shape((2, GROUP, POINTS), BF16)] * 4,
        grid=(2, 2),
        in_specs=[pl.BlockSpec((1, 1, 16, NS), lambda i, j: (freq, i, j, 0))],
        out_specs=[pl.BlockSpec((1, 16, POINTS), lambda i, j: (i, j, 0))] * 4,
        name=f"pack{freq}",
        cost_estimate=pl.CostEstimate(flops=0, bytes_accessed=4 << 20, transcendentals=0),
    )(sources)


def ring_gather(block, axis):
    half = block.shape[0] // 2
    below = ring_shift(block, axis, 1)
    above = ring_shift(block, axis, -1)
    far_low = ring_shift(below[:half], axis, 1)
    far_high = ring_shift(above[half:], axis, -1)
    return below, above, far_low, far_high


def gather_kernel(kernel):
    real = kernel[:, 0]
    imag = kernel[:, 1]
    rb, ra, rl, rh = ring_gather(real, "z")
    real_far = (rl[0], rh[0])
    imag_sets = []
    real_pieces = []
    for f in range(2):
        b, a, low, high = ring_gather(imag[f], PLANE[f])
        imag_sets.append(jnp.stack([imag[f], b, a, jnp.concatenate([low, high], 0)], 0))
        mine = jnp.stack([real[f], rb[f], ra[f], real_far[f]], 0)
        real_pieces.append((mine,) + ring_gather(mine, PLANE[f]))
    stacked = jnp.stack(imag_sets, 0)
    ib, ia, il, ih = ring_gather(stacked, "z")
    return [
        real_pieces[f] + (stacked, ib, ia, (il, ih)[f]) for f in range(2)
    ]


def kernel_specs(freq):
    four = pl.BlockSpec((4, RW, BLOCK), lambda i: (0, 0, 0))
    two = pl.BlockSpec((2, RW, BLOCK), lambda i: (0, 0, 0))
    pick = pl.BlockSpec((1, 4, RW, BLOCK), lambda i: (freq, 0, 0, 0))
    last = pl.BlockSpec((1, 4, RW, BLOCK), lambda i: (0, 0, 0, 0))
    return [four, four, four, two, two, pick, pick, pick, last]


def kernel_tiles(refs, dz, dp):
    r0, r1, r2, r3a, r3b, i0, i1, i2, i3 = refs
    if dp < 3:
        real = (r0, r1, r2)[dp][dz]
    elif dz < 2:
        real = r3a[dz]
    else:
        real = r3b[dz - 2]
    return real, (i0, i1, i2, i3)[dz][0, dp]


def full(dims):
    return pl.BlockSpec(dims, lambda i: (0,) * len(dims))


def forward_body(freq, *refs):
    xs, kern, outs, acc = refs[:4], refs[4:13], refs[13:17], refs[17]
    z = lax.axis_index("z")
    plane = lax.axis_index(PLANE[freq])
    form = (((1,), (1,)), ((), ()))
    first = True
    for dz in range(4):
        for dp in range(4):
            block = wrap(z, OFFSETS[dz]) * SIDE + wrap(plane, OFFSETS[dp])
            at = pl.ds(pl.multiple_of(block * BLOCK, BLOCK), BLOCK)
            rows = jnp.concatenate([x[part, :, at] for x in xs for part in range(2)], 0)
            for half, tile in enumerate(kernel_tiles(kern, dz, dp)):
                term = lax.dot_general(rows, tile, form, preferred_element_type=F32)
                cols = slice(half * RW, half * RW + RW)
                if first:
                    acc[:, cols] = term
                else:
                    acc[:, cols] += term
            first = False
    for g, out in enumerate(outs):
        xr = slice(g * 64, g * 64 + 32)
        xi = slice(g * 64 + 32, g * 64 + 64)
        out[0] = (acc[xr, :RW] - acc[xi, RW:]).astype(out.dtype)
        out[1] = (acc[xi, :RW] + acc[xr, RW:]).astype(out.dtype)


def forward(freq, xs, kern):
    part = (2, GROUP, RW)
    return call(
        functools.partial(forward_body, freq),
        [shape(part, F32)] + [shape(part, BF16)] * 3,
        grid=(1,),
        in_specs=[full((2, GROUP, POINTS))] * 4 + kernel_specs(freq),
        out_specs=[full(part)] * 4,
        scratch_shapes=[pltpu.VMEM((256, 2 * RW), F32)],
        name=f"forward{freq}",
        cost_estimate=pl.CostEstimate(flops=1 << 30, bytes_accessed=6 << 20, transcendentals=0),
    )(*xs, *kern)


def split_body(*refs):
    ins, keep, give = refs[:8], refs[8], refs[9]
    core = lax.axis_index("freq")
    for f in range(2):
        own, a, b, c = ins[4 * f : 4 * f + 4]
        for part in range(2):
            total = own[part] + a[part].astype(F32)
            total = total + b[part].astype(F32) + c[part].astype(F32)
            low = total[:, :128]
            high = total[:, 128:]
            keep[f, part] = jnp.where(core == 0, low, high).astype(BF16)
            give[f, part] = jnp.where(core == 0, high, low).astype(BF16)


def time_body(cos_ref, sin_ref, start_ref, stop_ref, mine_ref, other_ref, obs_ref, misfit_ref, keep_ref, give_ref):
    core = lax.axis_index("freq")
    samples = obs_ref.shape[0]
    first = start_ref[...]
    last = stop_ref[...]
    scale = 0.5
    for tile in range(2):
        rows = slice(tile * 16, tile * 16 + 16)
        fields = []
        for ref in (mine_ref, other_ref):
            for f in range(2):
                for part in range(2):
                    fields.append(ref[f, part, rows].astype(F32))

        def step(t, totals):
            coefs = []
            for side in (core, 1 - core):
                for f in range(2):
                    at = t * 4 + side * 2 + f
                    coefs.append(cos_ref[at])
                    coefs.append(-sin_ref[at])
            signal = coefs[0] * fields[0]
            for c, v in zip(coefs[1:], fields[1:]):
                signal = signal + c * v
            inside = (t >= first) & (t < last)
            gate = jnp.where(inside, 1.0, 0.0)
            rest = gate * (scale * signal - obs_ref[t, rows])
            misfit_ref[t, rows] = rest
            return tuple(total + c * rest for c, total in zip(coefs, totals))

        zero = jnp.zeros((16, 128), F32)
        totals = lax.fori_loop(0, samples, step, (zero,) * 8)
        for f in range(2):
            for part in range(2):
                keep_ref[f, part, rows] = (scale * totals[2 * f + part]).astype(BF16)
                give_ref[f, part, rows] = (scale * totals[4 + 2 * f + part]).astype(BF16)


def join_body(keep_ref, got_ref, *outs):
    core = lax.axis_index("freq")
    for f in range(2):
        for part in range(2):
            mine = keep_ref[f, part]
            got = got_ref[f, part]
            outs[f][part, :, :128] = jnp.where(core == 0, mine, got)
            outs[f][part, :, 128:] = jnp.where(core == 0, got, mine)


def adjoint_body(freq, *refs):
    bs, kern, outs = refs[:4], refs[4:13], refs[13:17]
    z = lax.axis_index("z")
    plane = lax.axis_index(PLANE[freq])
    form = (((1,), (0,)), ((), ()))
    left = jnp.concatenate([b[part] for b in bs for part in (0, 1)], 0)
    right = jnp.concatenate([b[1] if part == 0 else -b[0] for b in bs for part in (0, 1)], 0)
    factor = (NS / RW) ** 0.5
    for dz in range(4):
        for dp in range(4):
            block = wrap(z, OFFSETS[dz]) * SIDE + wrap(plane, OFFSETS[dp])
            at = pl.ds(pl.multiple_of(block * BLOCK, BLOCK), BLOCK)
            real, imag = kernel_tiles(kern, dz, dp)
            total = lax.dot_general(left, real, form, preferred_element_type=F32)
            total = total + lax.dot_general(right, imag, form, preferred_element_type=F32)
            total = (factor * total).astype(BF16)
            for g, out in enumerate(outs):
                for part in range(2):
                    row = g * 64 + part * 32
                    out[part, :, at] = total[row : row + 32]


def adjoint(freq, bs, kern):
    piece = (2, GROUP, POINTS)
    return call(
        functools.partial(adjoint_body, freq),
        [shape(piece, BF16)] * 4,
        grid=(1,),
        in_specs=[full((2, GROUP, RW))] * 4 + kernel_specs(freq),
        out_specs=[full(piece)] * 4,
        name=f"adjoint{freq}",
        cost_estimate=pl.CostEstimate(flops=1 << 30, bytes_accessed=6 << 20, transcendentals=0),
    )(*bs, *kern)


def merge_body(*refs):
    out = refs[8]
    for f in range(2):
        here = lax.axis_index(EXCHANGE[f])
        for step, piece in zip(OFFSETS, refs[4 * f : 4 * f + 4]):
            there = wrap(here, step)
            for z in range(SIDE):
                for plane in range(SIDE):
                    at = (z * SIDE + plane) * BLOCK
                    dst = column(f, z, plane, there)
                    out[f, 0, :, pl.ds(dst, BLOCK)] = piece[0, :, at : at + BLOCK]


def merge(pieces):
    return call(
        merge_body,
        shape((2, 2, GROUP, NS), BF16),
        grid=(2, 2),
        in_specs=[pl.BlockSpec((1, 16, POINTS), lambda i, j: (i, j, 0))] * 8,
        out_specs=pl.BlockSpec((2, 1, 16, NS), lambda i, j: (0, i, j, 0)),
        name="merge",
        cost_estimate=pl.CostEstimate(flops=0, bytes_accessed=8 << 20, transcendentals=0),
    )(*pieces)


def transform_tables(count, samples):
    sample_index = jnp.arange(samples, dtype=jnp.int32)
    bin_index = samples // 4 + jnp.arange(count, dtype=jnp.int32)
    phase = sample_index[:, None] * bin_index[None, :] % samples
    theta = 2.0 * jnp.pi / samples * phase.astype(F32)
    return jnp.cos(theta), jnp.sin(theta)


def collect(own, axis, give_low, give_high, give_far):
    return (
        own,
        ring_shift(give_high, axis, 1),
        ring_shift(give_low, axis, -1),
        ring_shift(give_far, axis, 2),
    )


def local(kernel, sources, observed, gate_start, gate_length):
    samples = observed.shape[1]
    xs = []
    for f in range(2):
        own, up, down, far = pack(sources, f)
        xs.append(collect(own, EXCHANGE[f], down, up, far))
    kern = gather_kernel(kernel)

    sums = []
    for f in range(2):
        own, low, high, far = forward(f, xs[f], kern[f])
        sums.extend(collect(own, EXCHANGE[f], low, high, far))
    half = shape((2, 2, GROUP, 128), BF16)
    mine, give = call(split_body, [half, half], name="split")(*sums)
    swap = [(0, 1), (1, 0)]
    other = lax.ppermute(give, "freq", swap)

    cosine, sine = transform_tables(4, samples)
    start = gate_start.reshape(1, 128)
    stop = (gate_start + gate_length).reshape(1, 128)
    vmem = pl.BlockSpec(memory_space=pltpu.VMEM)
    smem = pl.BlockSpec(memory_space=pltpu.SMEM)
    misfit, keep, give = call(
        time_body,
        [shape((samples, GROUP, 128), F32), half, half],
        in_specs=[smem, smem] + [vmem] * 5,
        out_specs=[vmem] * 3,
        name="time",
    )(
        cosine.reshape(-1),
        sine.reshape(-1),
        start,
        stop,
        mine,
        other,
        observed.transpose(1, 2, 0),
    )
    got = lax.ppermute(give, "freq", swap)
    whole = shape((2, GROUP, RW), BF16)
    backs = call(join_body, [whole, whole], name="join")(keep, got)

    pieces = []
    for f in range(2):
        b = backs[f]
        own, low, high, far = adjoint(f, collect(b, EXCHANGE[f], b, b, b), kern[f])
        pieces.extend(collect(own, EXCHANGE[f], low, high, far))
    gradient = merge(pieces)
    return gradient, misfit.transpose(2, 0, 1)


def solution(mesh):
    cube = Mesh(mesh.devices.reshape(2, SIDE, SIDE, SIDE), ("freq", "z", "y", "x"))
    vs = ("z", "y", "x")
    return jax.shard_map(
        local,
        mesh=cube,
        in_specs=(
            P("freq", None, None, vs),
            P("freq", None, vs, None),
            P("freq", None, vs),
            P("freq"),
            P("freq"),
        ),
        out_specs=(P("freq", None, vs, None), P("freq", None, vs)),
        check_vma=False,
    )
```
